128 devices in a mesh: dev: 128 (over z, y, x, core).
Axes of the slice: x: 4, y: 4, z: 4, core: 2. Of those that a mesh axis runs over, the one named last changes fastest.
Arguments:
- samples: bfloat16 [1024, 201216], P('dev'), may hold values from -6 to 6
- input_gain: float32 [1024], P('dev'), may hold values from 0.3 to 4, as said below
Outputs:
- visibility: bfloat16 [768, 36, 2, 128, 128], P('dev')
The draws below stay inside these ranges and needn't reach their ends.
Inputs may be any that keep to these rules, and one draw needn't show every extreme that they name: `input_gain`: positive gains, one for each input.
All inputs are finite; a program needn't handle non-finite values.
Results may differ from the reference program's by a relative error of at most 0.0071.
Values may be sent and summed in bfloat16 or wider, within the bound.
No kernel may reach another device: no remote copies, remote signals or barrier semaphores. Data moves between devices by JAX's collectives and lax.ppermute only.
A program may use at most 128 MiB of HBM per device.

```python
import math
import jax
import jax.numpy as jnp
import numpy as np
from jax import lax

INPUTS = 1024
FRAME = 1536
TAPS = 4
SPECTRA = 128
BLOCK = 128
CHANNELS = 768


def draw_input_gain(key, part):
    position = jnp.arange(INPUTS, dtype=jnp.int32).astype(jnp.float32) / max(INPUTS - 1, 1)
    rising = jnp.exp(0.5 * jnp.log(3.0) * position)
    spread = jnp.exp(jax.random.uniform(key, (INPUTS,), jnp.float32, jnp.log(0.7), jnp.log(1.4)))
    return (rising * spread).astype(jnp.float32)


def level_of(own_key, extent, shards, smallest, largest):
    loudness = 1.0
    for dim, parts in shards:
        steps = jax.random.uniform(jax.random.fold_in(jax.random.fold_in(own_key, 6), dim), (parts,), jnp.float32, smallest / len(shards), largest / len(shards))
        loudness = loudness * jnp.repeat(jnp.exp(steps), extent[dim] // parts).reshape((-1,) + (1,) * (len(extent) - 1 - dim))
    return loudness


def gaussian(own_key, extent, deviation, limit, cuts=(), kind=jnp.bfloat16):
    gain = level_of(own_key, extent, cuts, -0.22, 0.18) if cuts else 1.0
    drawn = jax.random.normal(own_key, extent, jnp.float32) * deviation * gain
    return jnp.minimum(jnp.maximum(drawn, -limit), limit).astype(kind)


def setup_inputs(seed: int = 0) -> dict:
    key_of = jax.random.split(jax.random.key(seed), 3)
    samples = gaussian(key_of[0], (INPUTS, (SPECTRA + TAPS - 1) * FRAME), 1.0, 6.0, ((0, 128),))
    input_gain = draw_input_gain(jax.random.fold_in(key_of[2], 71), 0)
    return dict(samples=samples, input_gain=input_gain)


def pfb_window():
    total = TAPS * FRAME
    position = jnp.arange(total, dtype=jnp.int32).astype(jnp.float32)
    centred = (position - total / 2 + 0.5) / FRAME
    taper = 0.54 - 0.46 * jnp.cos(2.0 * math.pi * position / (total - 1))
    return (jnp.sinc(centred) * taper).reshape(TAPS, FRAME)

def dft_table():
    sample_idx = jnp.arange(FRAME, dtype=jnp.int32)
    chan_idx = jnp.arange(CHANNELS, dtype=jnp.int32)
    phase = sample_idx[:, None] * chan_idx[None, :] % FRAME
    angle = 2.0 * math.pi / FRAME * phase.astype(jnp.float32)
    norm_factor = 1.0 / math.sqrt(FRAME)
    table = jnp.concatenate([jnp.cos(angle), -jnp.sin(angle)], axis=1) * norm_factor
    return table.astype(jnp.bfloat16)

def reference(samples, input_gain):
    window = pfb_window()
    table = dft_table()
    group = math.gcd(INPUTS, 64)
    frames = samples.reshape(INPUTS // group, group, SPECTRA + TAPS - 1, FRAME)
    gains = input_gain.reshape(INPUTS // group, group)

    def filter_group(args):
        block_frames, block_gain = args
        acc = jnp.zeros((group, SPECTRA, FRAME), jnp.float32)
        for tap in range(TAPS):
            acc = acc + window[tap][None, None, :] * block_frames[:, tap:tap + SPECTRA, :].astype(jnp.float32)
        filtered = acc.astype(jnp.bfloat16).reshape(group * SPECTRA, FRAME)
        spec = jnp.dot(filtered, table, preferred_element_type=jnp.float32)
        return spec.reshape(group, SPECTRA, 2 * CHANNELS) * block_gain[:, None, None]
    spectrum = lax.map(filter_group, (frames, gains)).reshape(INPUTS, SPECTRA, 2, CHANNELS)
    power = lax.optimization_barrier(jnp.sum(spectrum * spectrum, axis=(0, 1, 2)))
    level = 1.0 / jnp.sqrt(power / (INPUTS * SPECTRA) + 1e-06)
    quantized = (spectrum * level[None, None, None, :]).astype(jnp.bfloat16)
    per_channel = quantized.transpose(3, 0, 2, 1).reshape(CHANNELS, INPUTS, 2 * SPECTRA)
    nblk = INPUTS // BLOCK
    rows_np, cols_np = np.triu_indices(nblk)
    rows_idx = jnp.asarray(rows_np.astype(np.int32))
    cols_idx = jnp.asarray(cols_np.astype(np.int32))

    def one_channel(chan):
        tiles = chan.astype(jnp.float32).reshape(nblk, BLOCK, 2 * SPECTRA)
        left = jnp.take(tiles, rows_idx, axis=0)
        right = jnp.take(tiles, cols_idx, axis=0)
        turned = jnp.concatenate([-right[..., SPECTRA:], right[..., :SPECTRA]], axis=-1)
        real_part = jnp.einsum('pis,pjs->pij', left, right, precision=lax.Precision.HIGHEST)
        imag_part = jnp.einsum('pis,pjs->pij', left, turned, precision=lax.Precision.HIGHEST)
        stacked = jnp.stack([real_part, imag_part], axis=1) * (1.0 / SPECTRA)
        return stacked.astype(jnp.bfloat16)
    return lax.map(one_channel, per_channel)
```

```python
import functools
import math

import jax
import jax.numpy as jnp
import numpy as np
from jax import lax
from jax.experimental import pallas as pl
from jax.experimental.pallas import tpu as pltpu
from jax.sharding import PartitionSpec as P

INPUTS = 1024
FRAME = 1536
TAPS = 4
SPECTRA = 128
BLOCK = 128
CHANNELS = 768
DEVICES = 128
LOCAL = INPUTS // DEVICES
OWNED = CHANNELS // DEVICES
HALF = FRAME // 2
NBLK = INPUTS // BLOCK
SCALE = 1024.0
F32 = jnp.float32
BF16 = jnp.bfloat16
NT = (((1,), (1,)), ((), ()))


def pfb_window():
    total = TAPS * FRAME
    position = np.arange(total, dtype=np.float64)
    centred = (position - total / 2 + 0.5) / FRAME
    taper = 0.54 - 0.46 * np.cos(2.0 * math.pi * position / (total - 1))
    return (np.sinc(centred) * taper).reshape(TAPS, FRAME).astype(np.float32)


def twiddles():
    owner = np.outer(np.arange(DEVICES), np.arange(256)) % 256 * (2.0 * math.pi / 256)
    own = np.outer(np.arange(OWNED), np.arange(HALF)) % FRAME * (2.0 * math.pi / FRAME)
    norm = 1.0 / math.sqrt(FRAME)
    coarse = np.stack([np.cos(owner), -np.sin(owner)]) * norm
    fine = np.stack([np.cos(own), -np.sin(own)])
    return coarse.astype(np.float32), fine.astype(np.float32)


def make_table(parity, coarse_ref, fine_ref, table_ref):
    for block in range(HALF // 256):
        lanes = slice(block * 256, block * 256 + 256)
        re = coarse_ref[0]
        im = coarse_ref[1]
        for m in range(OWNED // 2):
            j = 2 * m + parity
            fre = fine_ref[0, j : j + 1, lanes]
            fim = fine_ref[1, j : j + 1, lanes]
            base = m * 2 * DEVICES
            table_ref[base : base + DEVICES, lanes] = (re * fre - im * fim).astype(BF16)
            table_ref[base + DEVICES : base + 2 * DEVICES, lanes] = (re * fim + im * fre).astype(BF16)


def transform(table_ref, folded_ref, gain_ref, out_ref, turned_ref):
    for pair in range(LOCAL // 2):
        rows = folded_ref[pair * 256 : pair * 256 + 256, :]
        for m in range(OWNED // 2):
            base = m * 2 * DEVICES
            spec = lax.dot_general(table_ref[base : base + 2 * DEVICES, :], rows, NT, preferred_element_type=F32)
            for side in range(2):
                i = 2 * pair + side
                gain = gain_ref[i] * SCALE
                for ri in range(2):
                    turned_ref[ri, pl.ds(m * LOCAL + i, DEVICES, stride=3 * LOCAL)] = (
                        spec[ri * DEVICES : (ri + 1) * DEVICES, side * SPECTRA : (side + 1) * SPECTRA] * gain
                    )
    for ri in range(2):
        out_ref[..., ri * SPECTRA : (ri + 1) * SPECTRA] = turned_ref[ri].reshape(DEVICES, OWNED // 2, LOCAL, SPECTRA).astype(BF16)


def filter_kernel(frames_ref, window_ref, coarse_ref, fine_ref, gain_ref, out_ref, odd_ref, even_ref, sum_ref, dif_ref, table_ref, turned_ref):
    step = 16
    width = 128

    def body(b, carry):
        s0 = b * step
        for block in range(HALF // width):
            acc = []
            for half in range(2):
                lanes = slice(half * HALF + block * width, half * HALF + block * width + width)
                frames = frames_ref[pl.ds(s0, step + TAPS - 1), :, lanes].astype(F32)
                total = window_ref[0, lanes][None, None, :] * frames[0:step]
                for tap in range(1, TAPS):
                    total = total + window_ref[tap, lanes][None, None, :] * frames[tap : tap + step]
                acc.append(total.reshape(step * LOCAL, width))
            here = pl.ds(pl.multiple_of(s0 * LOCAL, step * LOCAL), step * LOCAL)
            sum_ref[block, here] = acc[0] + acc[1]
            dif_ref[block, here] = acc[0] - acc[1]
        return carry

    lax.fori_loop(0, SPECTRA // step, body, 0)
    make_table(0, coarse_ref, fine_ref, table_ref)
    for i in range(LOCAL):
        for block in range(HALF // width):
            lanes = slice(block * width, block * width + width)
            mine = slice(i * SPECTRA, (i + 1) * SPECTRA)
            even_ref[mine, lanes] = sum_ref[block, pl.ds(i, SPECTRA, stride=LOCAL)].astype(BF16)
            odd_ref[mine, lanes] = dif_ref[block, pl.ds(i, SPECTRA, stride=LOCAL)].astype(BF16)
    transform(table_ref, even_ref, gain_ref, out_ref, turned_ref)


def odd_kernel(odd_ref, coarse_ref, fine_ref, gain_ref, out_ref, table_ref, turned_ref):
    make_table(1, coarse_ref, fine_ref, table_ref)
    transform(table_ref, odd_ref, gain_ref, out_ref, turned_ref)


def gram_kernel(spectra_ref, *refs):
    out_ref = refs[-1]
    volt = spectra_ref[...].reshape(INPUTS, 2 * SPECTRA)
    wide = volt.astype(F32)
    power = jnp.sum(wide * wide, keepdims=True) * (1.0 / (SCALE * SCALE))
    scale = (1.0 / (power / (INPUTS * SPECTRA) + 1e-06)) * (1.0 / (SCALE * SCALE * SPECTRA))
    for cols in range(NBLK // 2):
        right = volt[cols * 256 : cols * 256 + 256]
        turned = jnp.concatenate([-right[:, SPECTRA:], right[:, :SPECTRA]], axis=1)
        both = jnp.concatenate([right, turned], axis=0)
        height = (2 * cols + 2) * BLOCK
        tiles = lax.dot_general(volt[:height], both, NT, preferred_element_type=F32)
        tiles = (tiles * scale).astype(BF16)
        for r in range(2 * cols + 2):
            for side in range(2):
                c = 2 * cols + side
                if c < r:
                    continue
                p = r * NBLK - r * (r - 1) // 2 + c - r
                for ri in range(2):
                    at = ri * 256 + side * BLOCK
                    out_ref[p, ri] = tiles[r * BLOCK : (r + 1) * BLOCK, at : at + BLOCK]


def vmem(*shape):
    return pl.BlockSpec(memory_space=pltpu.VMEM)


def gram(parity, received, out=None):
    npair = NBLK * (NBLK + 1) // 2
    shape = jax.ShapeDtypeStruct((OWNED, npair, 2, BLOCK, BLOCK), BF16)
    args = [received]
    in_specs = [pl.BlockSpec((DEVICES, None, LOCAL, 2 * SPECTRA), lambda m: (0, m, 0, 0))]
    if out is not None:
        args.append(out)
        in_specs.append(pl.BlockSpec(memory_space=pl.ANY))
    return pl.pallas_call(
        gram_kernel,
        name=f"gram{parity}",
        grid=(OWNED // 2,),
        in_specs=in_specs,
        out_specs=pl.BlockSpec((None, npair, 2, BLOCK, BLOCK), lambda m: (2 * m + parity, 0, 0, 0, 0)),
        out_shape=shape,
        input_output_aliases={} if out is None else {1: 0},
        compiler_params=pltpu.CompilerParams(vmem_limit_bytes=48 << 20),
    )(*args)


def local(samples, input_gain):
    frames = samples.reshape(LOCAL, SPECTRA + TAPS - 1, FRAME).transpose(1, 0, 2)
    coarse, fine = (jnp.asarray(t) for t in twiddles())
    window = jnp.asarray(pfb_window())
    sent = jax.ShapeDtypeStruct((DEVICES, OWNED // 2, LOCAL, 2 * SPECTRA), BF16)
    rows = LOCAL * SPECTRA
    table = pltpu.VMEM((OWNED * DEVICES, HALF), BF16)
    turned = pltpu.VMEM((2, DEVICES * OWNED // 2 * LOCAL, SPECTRA), F32)
    folds = pltpu.VMEM((HALF // 128, rows, 128), F32)
    smem = pl.BlockSpec(memory_space=pltpu.SMEM)
    params = pltpu.CompilerParams(vmem_limit_bytes=48 << 20)
    even, folded = pl.pallas_call(
        filter_kernel,
        name="filter",
        in_specs=[vmem()] * 4 + [smem],
        out_specs=[vmem()] * 2,
        out_shape=[sent, jax.ShapeDtypeStruct((rows, HALF), BF16)],
        scratch_shapes=[pltpu.VMEM((rows, HALF), BF16), folds, folds, table, turned],
        compiler_params=params,
    )(frames, window, coarse, fine, input_gain)
    move = functools.partial(lax.all_to_all, axis_name="dev", split_axis=0, concat_axis=0, tiled=True)
    even = move(even)
    odd = pl.pallas_call(
        odd_kernel,
        name="odd",
        in_specs=[vmem()] * 3 + [smem],
        out_specs=vmem(),
        out_shape=sent,
        scratch_shapes=[table, turned],
        compiler_params=params,
    )(folded, coarse, fine, input_gain)
    odd = move(odd)
    return gram(1, odd, gram(0, even))


def solution(mesh):
    in_specs = (P("dev", None), P("dev"))
    out_specs = P("dev", None, None, None, None)
    return jax.shard_map(local, mesh=mesh, in_specs=in_specs, out_specs=out_specs, check_vma=False)
```

```python
import math

import jax
import jax.numpy as jnp
import numpy as np
from jax import lax
from jax.experimental import pallas as pl
from jax.experimental.pallas import tpu as pltpu
from jax.sharding import PartitionSpec as P

INPUTS = 1024
FRAME = 1536
TAPS = 4
SPECTRA = 128
BLOCK = 128
CHANNELS = 768
DEVICES = 128
LOCAL = INPUTS // DEVICES
OWNED = CHANNELS // DEVICES
HALF = FRAME // 2
NBLK = INPUTS // BLOCK
PER = OWNED // 2
STEP = 16
SCALE = 1024.0
F32 = jnp.float32
BF16 = jnp.bfloat16
NT = (((1,), (1,)), ((), ()))


def pfb_window():
    total = TAPS * FRAME
    position = np.arange(total, dtype=np.float64)
    centred = (position - total / 2 + 0.5) / FRAME
    taper = 0.54 - 0.46 * np.cos(2.0 * math.pi * position / (total - 1))
    return (np.sinc(centred) * taper).reshape(TAPS, FRAME).astype(np.float32)


def twiddles():
    owner = np.outer(np.arange(DEVICES), np.arange(256)) % 256 * (2.0 * math.pi / 256)
    own = np.outer(np.arange(OWNED), np.arange(HALF)) % FRAME * (2.0 * math.pi / FRAME)
    norm = 1.0 / math.sqrt(FRAME)
    coarse = np.stack([np.cos(owner), -np.sin(owner)]) * norm
    fine = np.stack([np.cos(own), -np.sin(own)])
    return coarse.astype(np.float32), fine.astype(np.float32)


def make_table(parity, coarse_ref, fine_ref, table_ref):
    for block in range(HALF // 256):
        lanes = slice(block * 256, block * 256 + 256)
        for m in range(PER):
            j = 2 * m + parity
            fre = fine_ref[0, j : j + 1, lanes]
            fim = fine_ref[1, j : j + 1, lanes]
            base = (parity * PER + m) * 2 * DEVICES
            re = coarse_ref[0]
            im = coarse_ref[1]
            table_ref[base : base + DEVICES, lanes] = (re * fre - im * fim).astype(BF16)
            table_ref[base + DEVICES : base + 2 * DEVICES, lanes] = (re * fim + im * fre).astype(BF16)


def frames_of(b, frames_hbm, frames_ref, sem):
    if b == 0:
        rows = pl.ds(0, STEP + TAPS - 1)
    else:
        rows = pl.ds(b * STEP + TAPS - 1, STEP)
    return pltpu.make_async_copy(frames_hbm.at[rows], frames_ref.at[rows], sem.at[b])


def transform_kernel(
    frames_hbm, window_hbm, coarse_hbm, fine_hbm, gain_ref, out_hbm,
    frames_ref, window_ref, coarse_ref, fine_ref, folds_ref, folded_ref, table_ref, turned_ref, sent_ref, frame_sem, sem, out_sem,
):
    small = [
        pltpu.make_async_copy(window_hbm, window_ref, sem.at[0]),
        pltpu.make_async_copy(coarse_hbm, coarse_ref, sem.at[1]),
        pltpu.make_async_copy(fine_hbm, fine_ref, sem.at[2]),
    ]
    for copy in small:
        copy.start()
    loads = [frames_of(b, frames_hbm, frames_ref, frame_sem) for b in range(SPECTRA // STEP)]
    for load in loads:
        load.start()
    for copy in small[1:]:
        copy.wait()
    for parity in range(2):
        make_table(parity, coarse_ref, fine_ref, table_ref)
    small[0].wait()
    width = 128

    def body(b):
        s0 = b * STEP
        for block in range(HALF // width):
            acc = []
            for half in range(2):
                lanes = slice(half * HALF + block * width, half * HALF + block * width + width)
                frames = frames_ref[pl.ds(s0, STEP + TAPS - 1), :, lanes].astype(F32)
                total = window_ref[0, lanes][None, None, :] * frames[0:STEP]
                for tap in range(1, TAPS):
                    total = total + window_ref[tap, lanes][None, None, :] * frames[tap : tap + STEP]
                acc.append(total.reshape(STEP * LOCAL, width))
            here = pl.ds(s0 * LOCAL, STEP * LOCAL)
            folds_ref[0, block, here] = acc[0] + acc[1]
            folds_ref[1, block, here] = acc[0] - acc[1]

    for b in range(SPECTRA // STEP):
        loads[b].wait()
        body(b)
    for i in range(LOCAL):
        for parity in range(2):
            for block in range(HALF // width):
                lanes = slice(block * width, block * width + width)
                mine = slice(i * SPECTRA, (i + 1) * SPECTRA)
                folded_ref[parity, mine, lanes] = folds_ref[parity, block, pl.ds(i, SPECTRA, stride=LOCAL)].astype(BF16)
    stores = []
    for parity in range(2):
        top = parity * PER * 2 * DEVICES
        for pair in range(LOCAL // 2):
            rows = folded_ref[parity, pair * 256 : pair * 256 + 256, :]
            spec = lax.dot_general(table_ref[top : top + PER * 2 * DEVICES, :], rows, NT, preferred_element_type=F32)
            for m in range(PER):
                for ri in range(2):
                    base = (m * 2 + ri) * DEVICES
                    for side in range(2):
                        i = 2 * pair + side
                        gain = gain_ref[i] * SCALE
                        turned_ref[parity, m, ri, pl.ds(i, DEVICES, stride=LOCAL)] = (
                            spec[base : base + DEVICES, side * SPECTRA : (side + 1) * SPECTRA] * gain
                        )
        for m in range(PER):
            c = parity * PER + m
            for ri in range(2):
                sent_ref[:, c, :, ri * SPECTRA : (ri + 1) * SPECTRA] = (
                    turned_ref[parity, m, ri].reshape(DEVICES, LOCAL, SPECTRA).astype(BF16)
                )
            store = pltpu.make_async_copy(sent_ref.at[:, c], out_hbm.at[:, c], out_sem.at[c])
            store.start()
            stores.append(store)
    for store in stores:
        store.wait()


def prepare(c, slot, spectra_ref, volt_ref, turn_ref, scale_ref):
    volt = spectra_ref[:, c].reshape(INPUTS, 2 * SPECTRA)
    volt_ref[slot] = volt
    turn_ref[slot, :, :SPECTRA] = -volt[:, SPECTRA:]
    turn_ref[slot, :, SPECTRA:] = volt[:, :SPECTRA]
    wide = volt.astype(F32)
    power = jnp.sum(wide * wide, keepdims=True) * (1.0 / (SCALE * SCALE))
    scale = (1.0 / (power / (INPUTS * SPECTRA) + 1e-06)) * (1.0 / (SCALE * SCALE * SPECTRA))
    scale_ref[slot] = jnp.broadcast_to(scale, (8, 128))


def gram_kernel(spectra_ref, out_ref, volt_ref, turn_ref, scale_ref):
    c = pl.program_id(0)
    slot = c % 2

    @pl.when(c == 0)
    def _():
        prepare(0, 0, spectra_ref, volt_ref, turn_ref, scale_ref)

    scale = scale_ref[slot][:1]
    for cols in range(NBLK // 2):
        height = (2 * cols + 2) * BLOCK
        at = slice(cols * 256, cols * 256 + 256)
        for ri, right_ref in enumerate((volt_ref, turn_ref)):
            tiles = lax.dot_general(volt_ref[slot, :height], right_ref[slot, at], NT, preferred_element_type=F32)
            for r in range(2 * cols + 2):
                for side in range(2):
                    col = 2 * cols + side
                    if col < r:
                        continue
                    p = r * NBLK - r * (r - 1) // 2 + col - r
                    tile = tiles[r * BLOCK : (r + 1) * BLOCK, side * BLOCK : (side + 1) * BLOCK]
                    out_ref[p, ri] = (tile * scale).astype(BF16)
    prepare(jnp.minimum(c + 1, OWNED - 1), 1 - slot, spectra_ref, volt_ref, turn_ref, scale_ref)


def gram(received):
    npair = NBLK * (NBLK + 1) // 2
    return pl.pallas_call(
        gram_kernel,
        name="gram",
        grid=(OWNED,),
        in_specs=[pl.BlockSpec(memory_space=pltpu.VMEM)],
        out_specs=pl.BlockSpec((None, npair, 2, BLOCK, BLOCK), lambda c: (2 * (c % PER) + c // PER, 0, 0, 0, 0)),
        out_shape=jax.ShapeDtypeStruct((OWNED, npair, 2, BLOCK, BLOCK), BF16),
        scratch_shapes=[
            pltpu.VMEM((2, INPUTS, 2 * SPECTRA), BF16),
            pltpu.VMEM((2, INPUTS, 2 * SPECTRA), BF16),
            pltpu.VMEM((2, 8, 128), F32),
        ],
        compiler_params=pltpu.CompilerParams(vmem_limit_bytes=48 << 20),
    )(received)


def local(samples, input_gain):
    frames = samples.reshape(LOCAL, SPECTRA + TAPS - 1, FRAME).transpose(1, 0, 2)
    coarse, fine = (jnp.asarray(t) for t in twiddles())
    window = jnp.asarray(pfb_window())
    rows = LOCAL * SPECTRA
    hbm = pl.BlockSpec(memory_space=pltpu.HBM)
    outgoing = pl.pallas_call(
        transform_kernel,
        name="transform",
        in_specs=[hbm] * 4 + [pl.BlockSpec(memory_space=pltpu.SMEM)],
        out_specs=hbm,
        out_shape=jax.ShapeDtypeStruct((DEVICES, OWNED, LOCAL, 2 * SPECTRA), BF16),
        scratch_shapes=[
            pltpu.VMEM(frames.shape, BF16),
            pltpu.VMEM(window.shape, F32),
            pltpu.VMEM(coarse.shape, F32),
            pltpu.VMEM(fine.shape, F32),
            pltpu.VMEM((2, HALF // 128, rows, 128), F32),
            pltpu.VMEM((2, rows, HALF), BF16),
            pltpu.VMEM((2 * OWNED * DEVICES, HALF), BF16),
            pltpu.VMEM((2, PER, 2, DEVICES * LOCAL, SPECTRA), F32),
            pltpu.VMEM((DEVICES, OWNED, LOCAL, 2 * SPECTRA), BF16),
            pltpu.SemaphoreType.DMA((SPECTRA // STEP,)),
            pltpu.SemaphoreType.DMA((3,)),
            pltpu.SemaphoreType.DMA((OWNED,)),
        ],
        compiler_params=pltpu.CompilerParams(vmem_limit_bytes=56 << 20),
    )(frames, window, coarse, fine, input_gain)
    return gram(lax.all_to_all(outgoing, "dev", split_axis=0, concat_axis=0, tiled=True))


def solution(mesh):
    in_specs = (P("dev", None), P("dev"))
    out_specs = P("dev", None, None, None, None)
    return jax.shard_map(local, mesh=mesh, in_specs=in_specs, out_specs=out_specs, check_vma=False)
```

```python
import math

import jax
import jax.numpy as jnp
import numpy as np
from jax import lax
from jax.experimental import pallas as pl
from jax.experimental.pallas import tpu as pltpu
from jax.sharding import PartitionSpec as P

INPUTS = 1024
FRAME = 1536
TAPS = 4
SPECTRA = 128
BLOCK = 128
CHANNELS = 768
DEVICES = 128
LOCAL = INPUTS // DEVICES
OWNED = CHANNELS // DEVICES
HALF = FRAME // 2
NBLK = INPUTS // BLOCK
PER = OWNED // 2
STEP = 16
PITCH = 9
SCALE = 1024.0
F32 = jnp.float32
BF16 = jnp.bfloat16
NT = (((1,), (1,)), ((), ()))


def pfb_window():
    total = TAPS * FRAME
    position = np.arange(total, dtype=np.float64)
    centred = (position - total / 2 + 0.5) / FRAME
    taper = 0.54 - 0.46 * np.cos(2.0 * math.pi * position / (total - 1))
    return (np.sinc(centred) * taper).reshape(TAPS, FRAME).astype(np.float32)


def dft_table():
    parity, m, owner = np.meshgrid(np.arange(2), np.arange(PER), np.arange(DEVICES), indexing="ij")
    channel = OWNED * owner + 2 * m + parity
    phase = channel[..., None] * np.arange(HALF) % FRAME
    angle = 2.0 * math.pi / FRAME * phase.astype(np.float64)
    table = np.stack([np.cos(angle), -np.sin(angle)], axis=2) / math.sqrt(FRAME)
    return table.reshape(2 * CHANNELS, HALF).astype(np.float32).astype(jnp.bfloat16)


def frames_of(b, frames_hbm, frames_ref, sem):
    if b == 0:
        rows = pl.ds(0, STEP + TAPS - 1)
    else:
        rows = pl.ds(b * STEP + TAPS - 1, STEP)
    return pltpu.make_async_copy(frames_hbm.at[rows], frames_ref.at[rows], sem.at[b])


def filter_pair(pair, raw_ref, window_ref, gain_ref, folded_ref):
    for side in range(2):
        i = 2 * pair + side
        gain = gain_ref[i] * SCALE
        for block in range(HALF // 128):
            acc = []
            for half in range(2):
                tile = half * (HALF // 128) + block
                lanes = slice(tile * 128, tile * 128 + 128)
                total = None
                for tap in range(TAPS):
                    weight = window_ref[tap : tap + 1, lanes] * gain
                    term = weight * raw_ref[tile, pl.ds(tap * PITCH + i, SPECTRA, stride=PITCH)]
                    total = term if total is None else total + term
                acc.append(total)
            lanes = slice(block * 128, block * 128 + 128)
            mine = slice(i * SPECTRA, (i + 1) * SPECTRA)
            folded_ref[0, mine, lanes] = (acc[0] + acc[1]).astype(BF16)
            folded_ref[1, mine, lanes] = (acc[0] - acc[1]).astype(BF16)


def transform_pair(pair, parity, table_ref, folded_ref, turned_ref):
    rows = folded_ref[parity, pair * 256 : pair * 256 + 256, :]
    top = parity * CHANNELS
    spec = lax.dot_general(table_ref[top : top + CHANNELS, :], rows, NT, preferred_element_type=F32)
    for m in range(PER):
        for ri in range(2):
            base = (m * 2 + ri) * DEVICES
            for side in range(2):
                turned_ref[parity * PER + m, ri, pl.ds(2 * pair + side, DEVICES, stride=PITCH)] = (
                    spec[base : base + DEVICES, side * SPECTRA : (side + 1) * SPECTRA]
                )


def pack(parity, turned_ref, sent_ref):
    for c in range(parity * PER, (parity + 1) * PER):
        for owner in range(DEVICES):
            for ri in range(2):
                rows = turned_ref[c, ri, owner * PITCH : owner * PITCH + LOCAL]
                sent_ref[owner, c, :, ri * SPECTRA : (ri + 1) * SPECTRA] = rows.astype(BF16)


def transform_kernel(
    frames_hbm, window_hbm, table_hbm, gain_ref, out_hbm,
    frames_ref, window_ref, table_ref, raw_ref, folded_ref, turned_ref, sent_ref, frame_sem, sem, out_sem,
):
    window_load = pltpu.make_async_copy(window_hbm, window_ref, sem.at[0])
    window_load.start()
    loads = [frames_of(b, frames_hbm, frames_ref, frame_sem) for b in range(SPECTRA // STEP)]
    for load in loads:
        load.start()
    table_load = pltpu.make_async_copy(table_hbm, table_ref, sem.at[1])
    table_load.start()
    for b, load in enumerate(loads):
        load.wait()
        first = b * STEP + TAPS - 1 if b else 0
        for f in range(first, (b + 1) * STEP + TAPS - 1):
            for tile in range(FRAME // 128):
                raw_ref[tile, f * PITCH : f * PITCH + LOCAL] = frames_ref[f, :, tile * 128 : tile * 128 + 128].astype(F32)
    window_load.wait()
    filter_pair(0, raw_ref, window_ref, gain_ref, folded_ref)
    table_load.wait()
    stores = []
    for pair in range(LOCAL // 2):
        transform_pair(pair, 0, table_ref, folded_ref, turned_ref)
        if pair + 1 < LOCAL // 2:
            filter_pair(pair + 1, raw_ref, window_ref, gain_ref, folded_ref)
        else:
            pack(0, turned_ref, sent_ref)
        transform_pair(pair, 1, table_ref, folded_ref, turned_ref)
    for parity in range(2):
        if parity:
            pack(parity, turned_ref, sent_ref)
        chans = pl.ds(parity * PER, PER)
        store = pltpu.make_async_copy(sent_ref.at[:, chans], out_hbm.at[:, chans], out_sem.at[parity])
        store.start()
        stores.append(store)
    for store in stores:
        store.wait()


def prepare(c, slot, spectra_ref, volt_ref, turn_ref, scale_ref):
    volt = spectra_ref[:, c].reshape(INPUTS, 2 * SPECTRA)
    volt_ref[slot] = volt
    turn_ref[slot, :, :SPECTRA] = -volt[:, SPECTRA:]
    turn_ref[slot, :, SPECTRA:] = volt[:, :SPECTRA]
    wide = volt.astype(F32)
    power = jnp.sum(wide * wide, keepdims=True) * (1.0 / (SCALE * SCALE))
    scale = (1.0 / (power / (INPUTS * SPECTRA) + 1e-06)) * (1.0 / (SCALE * SCALE * SPECTRA))
    scale_ref[slot] = jnp.broadcast_to(scale, (8, 128))


def gram_kernel(spectra_ref, out_ref, volt_ref, turn_ref, scale_ref):
    c = pl.program_id(0)
    slot = c % 2

    @pl.when(c == 0)
    def _():
        prepare(0, 0, spectra_ref, volt_ref, turn_ref, scale_ref)

    scale = scale_ref[slot][:1]
    for cols in range(NBLK // 2):
        height = (2 * cols + 2) * BLOCK
        at = slice(cols * 256, cols * 256 + 256)
        for ri, right_ref in enumerate((volt_ref, turn_ref)):
            tiles = lax.dot_general(volt_ref[slot, :height], right_ref[slot, at], NT, preferred_element_type=F32)
            for r in range(2 * cols + 2):
                for side in range(2):
                    col = 2 * cols + side
                    if col < r:
                        continue
                    p = r * NBLK - r * (r - 1) // 2 + col - r
                    tile = tiles[r * BLOCK : (r + 1) * BLOCK, side * BLOCK : (side + 1) * BLOCK]
                    out_ref[p, ri] = (tile * scale).astype(BF16)
    prepare(jnp.minimum(c + 1, OWNED - 1), 1 - slot, spectra_ref, volt_ref, turn_ref, scale_ref)


def gram(received):
    npair = NBLK * (NBLK + 1) // 2
    return pl.pallas_call(
        gram_kernel,
        name="gram",
        grid=(OWNED,),
        in_specs=[pl.BlockSpec(memory_space=pltpu.VMEM)],
        out_specs=pl.BlockSpec((None, npair, 2, BLOCK, BLOCK), lambda c: (2 * (c % PER) + c // PER, 0, 0, 0, 0)),
        out_shape=jax.ShapeDtypeStruct((OWNED, npair, 2, BLOCK, BLOCK), BF16),
        scratch_shapes=[
            pltpu.VMEM((2, INPUTS, 2 * SPECTRA), BF16),
            pltpu.VMEM((2, INPUTS, 2 * SPECTRA), BF16),
            pltpu.VMEM((2, 8, 128), F32),
        ],
        compiler_params=pltpu.CompilerParams(vmem_limit_bytes=48 << 20),
    )(received)


def local(samples, input_gain):
    frames = samples.reshape(LOCAL, SPECTRA + TAPS - 1, FRAME).transpose(1, 0, 2)
    table = jnp.asarray(dft_table())
    window = jnp.asarray(pfb_window())
    rows = LOCAL * SPECTRA
    hbm = pl.BlockSpec(memory_space=pltpu.HBM)
    outgoing = pl.pallas_call(
        transform_kernel,
        name="transform",
        in_specs=[hbm] * 3 + [pl.BlockSpec(memory_space=pltpu.SMEM)],
        out_specs=hbm,
        out_shape=jax.ShapeDtypeStruct((DEVICES, OWNED, LOCAL, 2 * SPECTRA), BF16),
        scratch_shapes=[
            pltpu.VMEM(frames.shape, BF16),
            pltpu.VMEM(window.shape, F32),
            pltpu.VMEM(table.shape, BF16),
            pltpu.VMEM((FRAME // 128, pl.cdiv(frames.shape[0] * PITCH, 8) * 8, 128), F32),
            pltpu.VMEM((2, rows, HALF), BF16),
            pltpu.VMEM((OWNED, 2, DEVICES * PITCH, SPECTRA), F32),
            pltpu.VMEM((DEVICES, OWNED, LOCAL, 2 * SPECTRA), BF16),
            pltpu.SemaphoreType.DMA((SPECTRA // STEP,)),
            pltpu.SemaphoreType.DMA((2,)),
            pltpu.SemaphoreType.DMA((2,)),
        ],
        compiler_params=pltpu.CompilerParams(vmem_limit_bytes=56 << 20),
    )(frames, window, table, input_gain)
    return gram(lax.all_to_all(outgoing, "dev", split_axis=0, concat_axis=0, tiled=True))


def solution(mesh):
    in_specs = (P("dev", None), P("dev"))
    out_specs = P("dev", None, None, None, None)
    return jax.shard_map(local, mesh=mesh, in_specs=in_specs, out_specs=out_specs, check_vma=False)
```

```python
import math

import jax
import jax.numpy as jnp
import numpy as np
from jax import lax
from jax.experimental import pallas as pl
from jax.experimental.pallas import tpu as pltpu
from jax.sharding import PartitionSpec as P

INPUTS = 1024
FRAME = 1536
TAPS = 4
SPECTRA = 128
BLOCK = 128
CHANNELS = 768
DEVICES = 128
LOCAL = INPUTS // DEVICES
OWNED = CHANNELS // DEVICES
HALF = FRAME // 2
NBLK = INPUTS // BLOCK
PER = OWNED // 2
STEP = 16
PITCH = 9
SCALE = 1024.0
F32 = jnp.float32
BF16 = jnp.bfloat16
NT = (((1,), (1,)), ((), ()))


def pfb_window():
    total = TAPS * FRAME
    position = np.arange(total, dtype=np.float64)
    centred = (position - total / 2 + 0.5) / FRAME
    taper = 0.54 - 0.46 * np.cos(2.0 * math.pi * position / (total - 1))
    return (np.sinc(centred) * taper).reshape(TAPS, FRAME).astype(np.float32)


def dft_table():
    parity, m, owner = np.meshgrid(np.arange(2), np.arange(PER), np.arange(DEVICES), indexing="ij")
    channel = OWNED * owner + 2 * m + parity
    phase = channel[..., None] * np.arange(HALF) % FRAME
    angle = 2.0 * math.pi / FRAME * phase.astype(np.float64)
    table = np.stack([np.cos(angle), -np.sin(angle)], axis=2) / math.sqrt(FRAME)
    return table.reshape(2 * CHANNELS, HALF).astype(np.float32).astype(jnp.bfloat16)


def frames_of(b, frames_hbm, frames_ref, sem):
    if b == 0:
        rows = pl.ds(0, STEP + TAPS - 1)
    else:
        rows = pl.ds(b * STEP + TAPS - 1, STEP)
    return pltpu.make_async_copy(frames_hbm.at[rows], frames_ref.at[rows], sem.at[b])


def filter_pair(pair, raw_ref, window_ref, gain_ref, folded_ref):
    for side in range(2):
        i = 2 * pair + side
        gain = gain_ref[i] * SCALE
        for block in range(HALF // 128):
            acc = []
            for half in range(2):
                tile = half * (HALF // 128) + block
                lanes = slice(tile * 128, tile * 128 + 128)
                total = None
                for tap in range(TAPS):
                    weight = window_ref[tap : tap + 1, lanes] * gain
                    term = weight * raw_ref[tile, pl.ds(tap * PITCH + i, SPECTRA, stride=PITCH)]
                    total = term if total is None else total + term
                acc.append(total)
            lanes = slice(block * 128, block * 128 + 128)
            mine = slice(i * SPECTRA, (i + 1) * SPECTRA)
            folded_ref[0, mine, lanes] = (acc[0] + acc[1]).astype(BF16)
            folded_ref[1, mine, lanes] = (acc[0] - acc[1]).astype(BF16)


def transform_pair(pair, parity, table_ref, folded_ref, turned_refs):
    rows = folded_ref[parity, pair * 256 : pair * 256 + 256, :]
    top = parity * CHANNELS
    spec = lax.dot_general(table_ref[top : top + CHANNELS, :], rows, NT, preferred_element_type=F32)
    for m in range(PER):
        for ri in range(2):
            base = (m * 2 + ri) * DEVICES
            for side in range(2):
                turned_refs[parity][m, ri, pl.ds(2 * pair + side, DEVICES, stride=PITCH)] = (
                    spec[base : base + DEVICES, side * SPECTRA : (side + 1) * SPECTRA]
                )


def pack(c, turned_refs, sent_refs, out_hbm, out_sem):
    turned_ref = turned_refs[c // PER]
    sent_ref = sent_refs[c // PER]
    m = c % PER
    for owner in range(DEVICES):
        for ri in range(2):
            rows = turned_ref[m, ri, owner * PITCH : owner * PITCH + LOCAL]
            sent_ref[owner, m, :, ri * SPECTRA : (ri + 1) * SPECTRA] = rows.astype(BF16)
    store = pltpu.make_async_copy(sent_ref.at[:, m], out_hbm.at[:, c], out_sem.at[c])
    store.start()
    return store


def transform_kernel(
    frames_hbm, window_hbm, table_hbm, gain_ref, out_hbm,
    frames_ref, window_ref, table_ref, raw_ref, folded_ref, turned_even, turned_odd, sent_even, sent_odd, frame_sem, sem, out_sem,
):
    turned_refs = (turned_even, turned_odd)
    sent_refs = (sent_even, sent_odd)
    window_load = pltpu.make_async_copy(window_hbm, window_ref, sem.at[0])
    window_load.start()
    loads = [frames_of(b, frames_hbm, frames_ref, frame_sem) for b in range(SPECTRA // STEP)]
    for load in loads:
        load.start()
    table_load = pltpu.make_async_copy(table_hbm, table_ref, sem.at[1])
    table_load.start()
    for b, load in enumerate(loads):
        load.wait()
        first = b * STEP + TAPS - 1 if b else 0
        for f in range(first, (b + 1) * STEP + TAPS - 1):
            for tile in range(FRAME // 128):
                raw_ref[tile, f * PITCH : f * PITCH + LOCAL] = frames_ref[f, :, tile * 128 : tile * 128 + 128].astype(F32)
    window_load.wait()
    filter_pair(0, raw_ref, window_ref, gain_ref, folded_ref)
    table_load.wait()
    stores = []
    for pair in range(LOCAL // 2):
        transform_pair(pair, 0, table_ref, folded_ref, turned_refs)
        if pair + 1 < LOCAL // 2:
            filter_pair(pair + 1, raw_ref, window_ref, gain_ref, folded_ref)
        else:
            for c in range(PER):
                stores.append(pack(c, turned_refs, sent_refs, out_hbm, out_sem))
        transform_pair(pair, 1, table_ref, folded_ref, turned_refs)
    for c in range(PER, OWNED):
        stores.append(pack(c, turned_refs, sent_refs, out_hbm, out_sem))
    for store in stores:
        store.wait()


def prepare(c, spectra_ref, volt_ref, turn_ref):
    slot = c % 2
    volt = spectra_ref[:, c].reshape(INPUTS, 2 * SPECTRA)
    volt_ref[slot] = volt
    turn_ref[slot, :, :SPECTRA] = -volt[:, SPECTRA:]
    turn_ref[slot, :, SPECTRA:] = volt[:, :SPECTRA]
    wide = volt.astype(F32)
    part = jnp.sum((wide * wide).reshape(8, INPUTS // 64, 8, 2 * SPECTRA), axis=1)
    power = jnp.sum(jnp.sum(part, axis=0), keepdims=True) * (1.0 / (SCALE * SCALE))
    return (1.0 / (power / (INPUTS * SPECTRA) + 1e-06)) * (1.0 / (SCALE * SCALE * SPECTRA))


def pair_of(row, col):
    return row * NBLK - row * (row - 1) // 2 + col - row


def gram_kernel(spectra_ref, out_hbm, volt_ref, turn_ref, tiles_ref, sem, last_sem):
    scale = prepare(0, spectra_ref, volt_ref, turn_ref)
    stores = []
    for c in range(OWNED):
        slot = c % 2
        channel = 2 * (c % PER) + c // PER
        following = None
        for cols in reversed(range(NBLK // 2)):
            height = (2 * cols + 2) * BLOCK
            at = slice(cols * 256, cols * 256 + 256)
            for ri, right_ref in enumerate((volt_ref, turn_ref)):
                tiles = lax.dot_general(volt_ref[slot, :height], right_ref[slot, at], NT, preferred_element_type=F32)
                for row in range(2 * cols + 2):
                    for side in range(2):
                        col = 2 * cols + side
                        if col >= row:
                            tile = tiles[row * BLOCK : (row + 1) * BLOCK, side * BLOCK : (side + 1) * BLOCK]
                            tiles_ref[c, pair_of(row, col), ri] = (tile * scale).astype(BF16)
            if following is None and c + 1 < OWNED:
                following = prepare(c + 1, spectra_ref, volt_ref, turn_ref)
            if c + 1 == OWNED:
                for row in range(2 * cols + 2):
                    first = max(row, 2 * cols)
                    pairs = pl.ds(pair_of(row, first), 2 * cols + 2 - first)
                    stores.append(pltpu.make_async_copy(tiles_ref.at[c, pairs], out_hbm.at[channel, pairs], last_sem.at[pair_of(row, first)]))
                    stores[-1].start()
        if c + 1 < OWNED:
            stores.append(pltpu.make_async_copy(tiles_ref.at[c], out_hbm.at[channel], sem.at[c]))
            stores[-1].start()
        scale = following
    for store in stores:
        store.wait()


def gram(received):
    shape = (OWNED, NBLK * (NBLK + 1) // 2, 2, BLOCK, BLOCK)
    return pl.pallas_call(
        gram_kernel,
        name="gram",
        in_specs=[pl.BlockSpec(memory_space=pltpu.VMEM)],
        out_specs=pl.BlockSpec(memory_space=pltpu.HBM),
        out_shape=jax.ShapeDtypeStruct(shape, BF16),
        scratch_shapes=[
            pltpu.VMEM((2, INPUTS, 2 * SPECTRA), BF16),
            pltpu.VMEM((2, INPUTS, 2 * SPECTRA), BF16),
            pltpu.VMEM(shape, BF16),
            pltpu.SemaphoreType.DMA((OWNED,)),
            pltpu.SemaphoreType.DMA(shape[1:2]),
        ],
        compiler_params=pltpu.CompilerParams(vmem_limit_bytes=48 << 20),
    )(received)


def local(samples, input_gain):
    frames = samples.reshape(LOCAL, SPECTRA + TAPS - 1, FRAME).transpose(1, 0, 2)
    table = jnp.asarray(dft_table())
    window = jnp.asarray(pfb_window())
    rows = LOCAL * SPECTRA
    hbm = pl.BlockSpec(memory_space=pltpu.HBM)
    outgoing = pl.pallas_call(
        transform_kernel,
        name="transform",
        in_specs=[hbm] * 3 + [pl.BlockSpec(memory_space=pltpu.SMEM)],
        out_specs=hbm,
        out_shape=jax.ShapeDtypeStruct((DEVICES, OWNED, LOCAL, 2 * SPECTRA), BF16),
        scratch_shapes=[
            pltpu.VMEM(frames.shape, BF16),
            pltpu.VMEM(window.shape, F32),
            pltpu.VMEM(table.shape, BF16),
            pltpu.VMEM((FRAME // 128, pl.cdiv(frames.shape[0] * PITCH, 8) * 8, 128), F32),
            pltpu.VMEM((2, rows, HALF), BF16),
            *[pltpu.VMEM((PER, 2, DEVICES * PITCH, SPECTRA), F32)] * 2,
            *[pltpu.VMEM((DEVICES, PER, LOCAL, 2 * SPECTRA), BF16)] * 2,
            pltpu.SemaphoreType.DMA((SPECTRA // STEP,)),
            pltpu.SemaphoreType.DMA((2,)),
            pltpu.SemaphoreType.DMA((OWNED,)),
        ],
        compiler_params=pltpu.CompilerParams(vmem_limit_bytes=56 << 20),
    )(frames, window, table, input_gain)
    return gram(lax.all_to_all(outgoing, "dev", split_axis=0, concat_axis=0, tiled=True))


def solution(mesh):
    in_specs = (P("dev", None), P("dev"))
    out_specs = P("dev", None, None, None, None)
    return jax.shard_map(local, mesh=mesh, in_specs=in_specs, out_specs=out_specs, check_vma=False)
```

```python
import math

import jax
import jax.numpy as jnp
import numpy as np
from jax import lax
from jax.experimental import pallas as pl
from jax.experimental.pallas import tpu as pltpu
from jax.sharding import PartitionSpec as P

INPUTS = 1024
FRAME = 1536
TAPS = 4
SPECTRA = 128
BLOCK = 128
CHANNELS = 768
DEVICES = 128
LOCAL = INPUTS // DEVICES
OWNED = CHANNELS // DEVICES
HALF = FRAME // 2
NBLK = INPUTS // BLOCK
PER = OWNED // 2
STEP = 16
PITCH = 9
SCALE = 1024.0
F32 = jnp.float32
BF16 = jnp.bfloat16
NT = (((1,), (1,)), ((), ()))


def pfb_window():
    total = TAPS * FRAME
    position = np.arange(total, dtype=np.float64)
    centred = (position - total / 2 + 0.5) / FRAME
    taper = 0.54 - 0.46 * np.cos(2.0 * math.pi * position / (total - 1))
    return (np.sinc(centred) * taper).reshape(TAPS, FRAME).astype(np.float32)


def dft_table():
    parity, m, owner = np.meshgrid(np.arange(2), np.arange(PER), np.arange(DEVICES), indexing="ij")
    channel = OWNED * owner + 2 * m + parity
    phase = channel[..., None] * np.arange(HALF) % FRAME
    angle = 2.0 * math.pi / FRAME * phase.astype(np.float64)
    table = np.stack([np.cos(angle), -np.sin(angle)], axis=2) / math.sqrt(FRAME)
    return table.reshape(2 * CHANNELS, HALF).astype(np.float32).astype(jnp.bfloat16)


def frames_of(b, frames_hbm, frames_ref, sem):
    if b == 0:
        rows = pl.ds(0, STEP + TAPS - 1)
    else:
        rows = pl.ds(b * STEP + TAPS - 1, STEP)
    return pltpu.make_async_copy(frames_hbm.at[rows], frames_ref.at[rows], sem.at[b])


def filter_pair(pair, raw_ref, window_ref, gain_ref, folded_ref):
    for side in range(2):
        i = 2 * pair + side
        gain = gain_ref[i] * SCALE
        for block in range(HALF // 128):
            acc = []
            for half in range(2):
                tile = half * (HALF // 128) + block
                lanes = slice(tile * 128, tile * 128 + 128)
                total = None
                for tap in range(TAPS):
                    weight = window_ref[tap : tap + 1, lanes] * gain
                    term = weight * raw_ref[tile, pl.ds(tap * PITCH + i, SPECTRA, stride=PITCH)]
                    total = term if total is None else total + term
                acc.append(total)
            lanes = slice(block * 128, block * 128 + 128)
            mine = slice(i * SPECTRA, (i + 1) * SPECTRA)
            folded_ref[0, mine, lanes] = (acc[0] + acc[1]).astype(BF16)
            folded_ref[1, mine, lanes] = (acc[0] - acc[1]).astype(BF16)


def transform_pair(pair, parity, table_ref, folded_ref, turned_refs):
    rows = folded_ref[parity, pair * 256 : pair * 256 + 256, :]
    top = parity * CHANNELS
    spec = lax.dot_general(table_ref[top : top + CHANNELS, :], rows, NT, preferred_element_type=F32)
    for m in range(PER):
        for ri in range(2):
            base = (m * 2 + ri) * DEVICES
            for side in range(2):
                turned_refs[parity][m, ri, pl.ds(2 * pair + side, DEVICES, stride=PITCH)] = (
                    spec[base : base + DEVICES, side * SPECTRA : (side + 1) * SPECTRA]
                )


def pack(c, turned_refs, sent_refs, out_hbm, out_sem):
    turned_ref = turned_refs[c // PER]
    sent_ref = sent_refs[c // PER]
    m = c % PER
    for owner in range(DEVICES):
        for ri in range(2):
            rows = turned_ref[m, ri, owner * PITCH : owner * PITCH + LOCAL]
            sent_ref[owner, m, :, ri * SPECTRA : (ri + 1) * SPECTRA] = rows.astype(BF16)
    store = pltpu.make_async_copy(sent_ref.at[:, m], out_hbm.at[:, c], out_sem.at[c])
    store.start()
    return store


def transform_kernel(
    frames_hbm, window_hbm, table_hbm, gain_hbm, out_hbm,
    gain_ref, frames_ref, window_ref, table_ref, raw_ref, folded_ref, turned_even, turned_odd, sent_even, sent_odd, frame_sem, sem, out_sem,
):
    turned_refs = (turned_even, turned_odd)
    sent_refs = (sent_even, sent_odd)
    window_load = pltpu.make_async_copy(window_hbm, window_ref, sem.at[0])
    window_load.start()
    gain_load = pltpu.make_async_copy(gain_hbm, gain_ref, sem.at[2])
    gain_load.start()
    loads = [frames_of(b, frames_hbm, frames_ref, frame_sem) for b in range(SPECTRA // STEP)]
    for load in loads:
        load.start()
    table_load = pltpu.make_async_copy(table_hbm, table_ref, sem.at[1])
    table_load.start()
    for b, load in enumerate(loads):
        load.wait()
        first = b * STEP + TAPS - 1 if b else 0
        for f in range(first, (b + 1) * STEP + TAPS - 1):
            for tile in range(FRAME // 128):
                raw_ref[tile, f * PITCH : f * PITCH + LOCAL] = frames_ref[f, :, tile * 128 : tile * 128 + 128].astype(F32)
    window_load.wait()
    gain_load.wait()
    filter_pair(0, raw_ref, window_ref, gain_ref, folded_ref)
    table_load.wait()
    stores = []
    for pair in range(LOCAL // 2):
        transform_pair(pair, 0, table_ref, folded_ref, turned_refs)
        if pair + 1 < LOCAL // 2:
            filter_pair(pair + 1, raw_ref, window_ref, gain_ref, folded_ref)
        else:
            for c in range(PER):
                stores.append(pack(c, turned_refs, sent_refs, out_hbm, out_sem))
        transform_pair(pair, 1, table_ref, folded_ref, turned_refs)
    for c in range(PER, OWNED):
        stores.append(pack(c, turned_refs, sent_refs, out_hbm, out_sem))
    for store in stores:
        store.wait()


def prepare(c, spectra_ref, volt_ref, turn_ref):
    slot = c % 2
    volt = spectra_ref[:, c].reshape(INPUTS, 2 * SPECTRA)
    volt_ref[slot] = volt
    turn_ref[slot, :, :SPECTRA] = -volt[:, SPECTRA:]
    turn_ref[slot, :, SPECTRA:] = volt[:, :SPECTRA]
    wide = volt.astype(F32)
    part = jnp.sum((wide * wide).reshape(8, INPUTS // 64, 8, 2 * SPECTRA), axis=1)
    power = jnp.sum(jnp.sum(part, axis=0), keepdims=True) * (1.0 / (SCALE * SCALE))
    return (1.0 / (power / (INPUTS * SPECTRA) + 1e-06)) * (1.0 / (SCALE * SCALE * SPECTRA))


def pair_of(row, col):
    return row * NBLK - row * (row - 1) // 2 + col - row


def gram_kernel(spectra_ref, out_hbm, volt_ref, turn_ref, tiles_ref, sem, last_sem):
    scale = prepare(0, spectra_ref, volt_ref, turn_ref)
    stores = []
    for c in range(OWNED):
        slot = c % 2
        channel = 2 * (c % PER) + c // PER
        following = None
        for cols in reversed(range(NBLK // 2)):
            height = (2 * cols + 2) * BLOCK
            at = slice(cols * 256, cols * 256 + 256)
            for ri, right_ref in enumerate((volt_ref, turn_ref)):
                tiles = lax.dot_general(volt_ref[slot, :height], right_ref[slot, at], NT, preferred_element_type=F32)
                for row in range(2 * cols + 2):
                    for side in range(2):
                        col = 2 * cols + side
                        if col >= row:
                            tile = tiles[row * BLOCK : (row + 1) * BLOCK, side * BLOCK : (side + 1) * BLOCK]
                            tiles_ref[c, pair_of(row, col), ri] = (tile * scale).astype(BF16)
            if following is None and c + 1 < OWNED:
                following = prepare(c + 1, spectra_ref, volt_ref, turn_ref)
            if c + 1 == OWNED:
                for row in range(2 * cols + 2):
                    first = max(row, 2 * cols)
                    pairs = pl.ds(pair_of(row, first), 2 * cols + 2 - first)
                    stores.append(pltpu.make_async_copy(tiles_ref.at[c, pairs], out_hbm.at[channel, pairs], last_sem.at[pair_of(row, first)]))
                    stores[-1].start()
        if c + 1 < OWNED:
            stores.append(pltpu.make_async_copy(tiles_ref.at[c], out_hbm.at[channel], sem.at[c]))
            stores[-1].start()
        scale = following
    for store in stores:
        store.wait()


def gram(received):
    shape = (OWNED, NBLK * (NBLK + 1) // 2, 2, BLOCK, BLOCK)
    return pl.pallas_call(
        gram_kernel,
        name="gram",
        in_specs=[pl.BlockSpec(memory_space=pltpu.VMEM)],
        out_specs=pl.BlockSpec(memory_space=pltpu.HBM),
        out_shape=jax.ShapeDtypeStruct(shape, BF16),
        scratch_shapes=[
            pltpu.VMEM((2, INPUTS, 2 * SPECTRA), BF16),
            pltpu.VMEM((2, INPUTS, 2 * SPECTRA), BF16),
            pltpu.VMEM(shape, BF16),
            pltpu.SemaphoreType.DMA((OWNED,)),
            pltpu.SemaphoreType.DMA(shape[1:2]),
        ],
        compiler_params=pltpu.CompilerParams(vmem_limit_bytes=48 << 20),
    )(received)


def local(samples, input_gain):
    frames = samples.reshape(LOCAL, SPECTRA + TAPS - 1, FRAME).transpose(1, 0, 2)
    table = jnp.asarray(dft_table())
    window = jnp.asarray(pfb_window())
    rows = LOCAL * SPECTRA
    hbm = pl.BlockSpec(memory_space=pltpu.HBM)
    outgoing = pl.pallas_call(
        transform_kernel,
        name="transform",
        in_specs=[hbm] * 4,
        out_specs=hbm,
        out_shape=jax.ShapeDtypeStruct((DEVICES, OWNED, LOCAL, 2 * SPECTRA), BF16),
        scratch_shapes=[
            pltpu.SMEM((LOCAL,), F32),
            pltpu.VMEM(frames.shape, BF16),
            pltpu.VMEM(window.shape, F32),
            pltpu.VMEM(table.shape, BF16),
            pltpu.VMEM((FRAME // 128, pl.cdiv(frames.shape[0] * PITCH, 8) * 8, 128), F32),
            pltpu.VMEM((2, rows, HALF), BF16),
            *[pltpu.VMEM((PER, 2, DEVICES * PITCH, SPECTRA), F32)] * 2,
            *[pltpu.VMEM((DEVICES, PER, LOCAL, 2 * SPECTRA), BF16)] * 2,
            pltpu.SemaphoreType.DMA((SPECTRA // STEP,)),
            pltpu.SemaphoreType.DMA((3,)),
            pltpu.SemaphoreType.DMA((OWNED,)),
        ],
        compiler_params=pltpu.CompilerParams(vmem_limit_bytes=56 << 20),
    )(frames, window, table, input_gain)
    return gram(lax.all_to_all(outgoing, "dev", split_axis=0, concat_axis=0, tiled=True))


def solution(mesh):
    in_specs = (P("dev", None), P("dev"))
    out_specs = P("dev", None, None, None, None)
    return jax.shard_map(local, mesh=mesh, in_specs=in_specs, out_specs=out_specs, check_vma=False)
```

```python
import math

import jax
import jax.numpy as jnp
import numpy as np
from jax import lax
from jax.experimental import pallas as pl
from jax.experimental.pallas import tpu as pltpu
from jax.sharding import PartitionSpec as P

INPUTS = 1024
FRAME = 1536
TAPS = 4
SPECTRA = 128
BLOCK = 128
CHANNELS = 768
DEVICES = 128
LOCAL = INPUTS // DEVICES
OWNED = CHANNELS // DEVICES
HALF = FRAME // 2
NBLK = INPUTS // BLOCK
PER = OWNED // 2
STEP = 32
PITCH = 9
SCALE = 1024.0
F32 = jnp.float32
BF16 = jnp.bfloat16
NT = (((1,), (1,)), ((), ()))


def pfb_window():
    total = TAPS * FRAME
    position = np.arange(total, dtype=np.float64)
    centred = (position - total / 2 + 0.5) / FRAME
    taper = 0.54 - 0.46 * np.cos(2.0 * math.pi * position / (total - 1))
    return (np.sinc(centred) * taper).reshape(TAPS, FRAME).astype(np.float32)


def dft_table():
    parity, m, owner = np.meshgrid(np.arange(2), np.arange(PER), np.arange(DEVICES), indexing="ij")
    channel = OWNED * owner + 2 * m + parity
    phase = channel[..., None] * np.arange(HALF) % FRAME
    angle = 2.0 * math.pi / FRAME * phase.astype(np.float64)
    table = np.stack([np.cos(angle), -np.sin(angle)], axis=2) / math.sqrt(FRAME)
    return table.reshape(2 * CHANNELS, HALF).astype(np.float32).astype(jnp.bfloat16)


def frames_of(b, frames_hbm, frames_ref, sem):
    if b == 0:
        rows = pl.ds(0, STEP + TAPS - 1)
    else:
        rows = pl.ds(b * STEP + TAPS - 1, STEP)
    return pltpu.make_async_copy(frames_hbm.at[rows], frames_ref.at[rows], sem.at[b])


def filter_pair(pair, raw_ref, window_ref, gain_ref, folded_ref):
    for side in range(2):
        i = 2 * pair + side
        gain = gain_ref[i] * SCALE
        for block in range(HALF // 128):
            acc = []
            for half in range(2):
                tile = half * (HALF // 128) + block
                lanes = slice(tile * 128, tile * 128 + 128)
                total = None
                for tap in range(TAPS):
                    weight = window_ref[tap : tap + 1, lanes] * gain
                    term = weight * raw_ref[tile, pl.ds(tap * PITCH + i, SPECTRA, stride=PITCH)]
                    total = term if total is None else total + term
                acc.append(total)
            lanes = slice(block * 128, block * 128 + 128)
            mine = slice(i * SPECTRA, (i + 1) * SPECTRA)
            folded_ref[0, mine, lanes] = (acc[0] + acc[1]).astype(BF16)
            folded_ref[1, mine, lanes] = (acc[0] - acc[1]).astype(BF16)


def transform_pair(pair, parity, table_ref, folded_ref, turned_refs):
    rows = folded_ref[parity, pair * 256 : pair * 256 + 256, :]
    top = parity * CHANNELS
    spec = lax.dot_general(table_ref[top : top + CHANNELS, :], rows, NT, preferred_element_type=F32)
    for m in range(PER):
        for ri in range(2):
            base = (m * 2 + ri) * DEVICES
            for side in range(2):
                turned_refs[parity][m, ri, pl.ds(2 * pair + side, DEVICES, stride=PITCH)] = (
                    spec[base : base + DEVICES, side * SPECTRA : (side + 1) * SPECTRA]
                )


def pack(c, turned_refs, sent_refs, out_hbm, out_sem):
    turned_ref = turned_refs[c // PER]
    sent_ref = sent_refs[c // PER]
    m = c % PER
    for owner in range(DEVICES):
        for ri in range(2):
            rows = turned_ref[m, ri, owner * PITCH : owner * PITCH + LOCAL]
            sent_ref[owner, m, :, ri * SPECTRA : (ri + 1) * SPECTRA] = rows.astype(BF16)
    store = pltpu.make_async_copy(sent_ref.at[:, m], out_hbm.at[:, c], out_sem.at[c])
    store.start()
    return store


def transform_kernel(
    frames_hbm, window_hbm, table_hbm, gain_hbm, out_hbm,
    gain_ref, frames_ref, window_ref, table_ref, raw_ref, folded_ref, turned_even, turned_odd, sent_even, sent_odd, frame_sem, sem, out_sem,
):
    turned_refs = (turned_even, turned_odd)
    sent_refs = (sent_even, sent_odd)
    window_load = pltpu.make_async_copy(window_hbm, window_ref, sem.at[0])
    window_load.start()
    gain_load = pltpu.make_async_copy(gain_hbm, gain_ref, sem.at[2])
    gain_load.start()
    loads = [frames_of(b, frames_hbm, frames_ref, frame_sem) for b in range(SPECTRA // STEP)]
    for load in loads:
        load.start()
    table_load = pltpu.make_async_copy(table_hbm, table_ref, sem.at[1])
    table_load.start()
    for b, load in enumerate(loads):
        load.wait()
        first = b * STEP + TAPS - 1 if b else 0
        for f in range(first, (b + 1) * STEP + TAPS - 1):
            for tile in range(FRAME // 128):
                raw_ref[tile, f * PITCH : f * PITCH + LOCAL] = frames_ref[f, :, tile * 128 : tile * 128 + 128].astype(F32)
    window_load.wait()
    gain_load.wait()
    filter_pair(0, raw_ref, window_ref, gain_ref, folded_ref)
    table_load.wait()
    stores = []
    for pair in range(LOCAL // 2):
        transform_pair(pair, 0, table_ref, folded_ref, turned_refs)
        if pair + 1 < LOCAL // 2:
            filter_pair(pair + 1, raw_ref, window_ref, gain_ref, folded_ref)
        else:
            for c in range(PER):
                stores.append(pack(c, turned_refs, sent_refs, out_hbm, out_sem))
        transform_pair(pair, 1, table_ref, folded_ref, turned_refs)
    for c in range(PER, OWNED):
        stores.append(pack(c, turned_refs, sent_refs, out_hbm, out_sem))
    for store in stores:
        store.wait()


def prepare(c, spectra_ref, volt_ref, turn_ref):
    slot = c % 2
    volt = spectra_ref[:, c].reshape(INPUTS, 2 * SPECTRA)
    volt_ref[slot] = volt
    turn_ref[slot, :, :SPECTRA] = -volt[:, SPECTRA:]
    turn_ref[slot, :, SPECTRA:] = volt[:, :SPECTRA]
    wide = volt.astype(F32)
    part = jnp.sum((wide * wide).reshape(8, INPUTS // 64, 8, 2 * SPECTRA), axis=1)
    power = jnp.sum(jnp.sum(part, axis=0), keepdims=True) * (1.0 / (SCALE * SCALE))
    return (1.0 / (power / (INPUTS * SPECTRA) + 1e-06)) * (1.0 / (SCALE * SCALE * SPECTRA))


def pair_of(row, col):
    return row * NBLK - row * (row - 1) // 2 + col - row


def gram_kernel(spectra_ref, out_hbm, volt_ref, turn_ref, tiles_ref, sem):
    scale = prepare(0, spectra_ref, volt_ref, turn_ref)
    stores = []
    for c in range(OWNED):
        slot = c % 2
        channel = 2 * (c % PER) + c // PER
        following = None
        for cols in reversed(range(NBLK // 2)):
            height = (2 * cols + 2) * BLOCK
            at = slice(cols * 256, cols * 256 + 256)
            for ri, right_ref in enumerate((volt_ref, turn_ref)):
                tiles = lax.dot_general(volt_ref[slot, :height], right_ref[slot, at], NT, preferred_element_type=F32)
                for row in range(2 * cols + 2):
                    for side in range(2):
                        col = 2 * cols + side
                        if col >= row:
                            tile = tiles[row * BLOCK : (row + 1) * BLOCK, side * BLOCK : (side + 1) * BLOCK]
                            tiles_ref[c, pair_of(row, col), ri] = (tile * scale).astype(BF16)
            if following is None and c + 1 < OWNED:
                following = prepare(c + 1, spectra_ref, volt_ref, turn_ref)
        stores.append(pltpu.make_async_copy(tiles_ref.at[c], out_hbm.at[channel], sem.at[c]))
        stores[-1].start()
        scale = following
    for store in stores:
        store.wait()


def gram(received):
    shape = (OWNED, NBLK * (NBLK + 1) // 2, 2, BLOCK, BLOCK)
    return pl.pallas_call(
        gram_kernel,
        name="gram",
        in_specs=[pl.BlockSpec(memory_space=pltpu.VMEM)],
        out_specs=pl.BlockSpec(memory_space=pltpu.HBM),
        out_shape=jax.ShapeDtypeStruct(shape, BF16),
        scratch_shapes=[
            pltpu.VMEM((2, INPUTS, 2 * SPECTRA), BF16),
            pltpu.VMEM((2, INPUTS, 2 * SPECTRA), BF16),
            pltpu.VMEM(shape, BF16),
            pltpu.SemaphoreType.DMA((OWNED,)),
        ],
        compiler_params=pltpu.CompilerParams(vmem_limit_bytes=48 << 20),
    )(received)


def local(samples, input_gain):
    frames = samples.reshape(LOCAL, SPECTRA + TAPS - 1, FRAME).transpose(1, 0, 2)
    table = jnp.asarray(dft_table())
    window = jnp.asarray(pfb_window())
    rows = LOCAL * SPECTRA
    hbm = pl.BlockSpec(memory_space=pltpu.HBM)
    outgoing = pl.pallas_call(
        transform_kernel,
        name="transform",
        in_specs=[hbm] * 4,
        out_specs=hbm,
        out_shape=jax.ShapeDtypeStruct((DEVICES, OWNED, LOCAL, 2 * SPECTRA), BF16),
        scratch_shapes=[
            pltpu.SMEM((LOCAL,), F32),
            pltpu.VMEM(frames.shape, BF16),
            pltpu.VMEM(window.shape, F32),
            pltpu.VMEM(table.shape, BF16),
            pltpu.VMEM((FRAME // 128, pl.cdiv(frames.shape[0] * PITCH, 8) * 8, 128), F32),
            pltpu.VMEM((2, rows, HALF), BF16),
            *[pltpu.VMEM((PER, 2, DEVICES * PITCH, SPECTRA), F32)] * 2,
            *[pltpu.VMEM((DEVICES, PER, LOCAL, 2 * SPECTRA), BF16)] * 2,
            pltpu.SemaphoreType.DMA((SPECTRA // STEP,)),
            pltpu.SemaphoreType.DMA((3,)),
            pltpu.SemaphoreType.DMA((OWNED,)),
        ],
        compiler_params=pltpu.CompilerParams(vmem_limit_bytes=56 << 20),
    )(frames, window, table, input_gain)
    return gram(lax.all_to_all(outgoing, "dev", split_axis=0, concat_axis=0, tiled=True))


def solution(mesh):
    in_specs = (P("dev", None), P("dev"))
    out_specs = P("dev", None, None, None, None)
    return jax.shard_map(local, mesh=mesh, in_specs=in_specs, out_specs=out_specs, check_vma=False)
```

```python
import math

import jax
import jax.numpy as jnp
import numpy as np
from jax import lax
from jax.experimental import pallas as pl
from jax.experimental.pallas import tpu as pltpu
from jax.sharding import PartitionSpec as P

INPUTS = 1024
FRAME = 1536
TAPS = 4
SPECTRA = 128
BLOCK = 128
CHANNELS = 768
DEVICES = 128
LOCAL = INPUTS // DEVICES
OWNED = CHANNELS // DEVICES
HALF = FRAME // 2
NBLK = INPUTS // BLOCK
PER = OWNED // 2
STEP = 32
PITCH = 9
SCALE = 1024.0
F32 = jnp.float32
BF16 = jnp.bfloat16
NT = (((1,), (1,)), ((), ()))


def pfb_window():
    total = TAPS * FRAME
    position = np.arange(total, dtype=np.float64)
    centred = (position - total / 2 + 0.5) / FRAME
    taper = 0.54 - 0.46 * np.cos(2.0 * math.pi * position / (total - 1))
    return (np.sinc(centred) * taper).reshape(TAPS, FRAME).astype(np.float32)


def twiddles():
    owner = np.outer(np.arange(DEVICES), np.arange(256)) % 256 * (2.0 * math.pi / 256)
    own = np.outer(np.arange(OWNED), np.arange(HALF)) % FRAME * (2.0 * math.pi / FRAME)
    coarse = np.stack([np.cos(owner), -np.sin(owner)]) / math.sqrt(FRAME)
    fine = np.stack([np.cos(own), -np.sin(own)])
    return coarse.astype(np.float32), fine.astype(np.float32)


def odd_table():
    m, owner = np.meshgrid(np.arange(PER), np.arange(DEVICES), indexing="ij")
    channel = OWNED * owner + 2 * m + 1
    angle = 2.0 * math.pi / FRAME * (channel[..., None] * np.arange(HALF) % FRAME)
    table = np.stack([np.cos(angle), -np.sin(angle)], axis=1) / math.sqrt(FRAME)
    return table.reshape(CHANNELS, HALF).astype(np.float32).astype(jnp.bfloat16)


def even_table(coarse_ref, fine_ref, table_ref):
    group = 32
    for top in range(0, DEVICES, group):
        re = coarse_ref[0, top : top + group]
        im = coarse_ref[1, top : top + group]
        for block in range(HALF // 256):
            lanes = slice(block * 256, block * 256 + 256)
            for m in range(PER):
                at = m * 2 * DEVICES + top
                if m == 0:
                    table_ref[at : at + group, lanes] = re.astype(BF16)
                    table_ref[at + DEVICES : at + DEVICES + group, lanes] = im.astype(BF16)
                    continue
                fre = fine_ref[0, 2 * m : 2 * m + 1, lanes]
                fim = fine_ref[1, 2 * m : 2 * m + 1, lanes]
                table_ref[at : at + group, lanes] = (re * fre - im * fim).astype(BF16)
                table_ref[at + DEVICES : at + DEVICES + group, lanes] = (re * fim + im * fre).astype(BF16)


def frames_of(b, frames_hbm, frames_ref, sem):
    if b == 0:
        rows = pl.ds(0, STEP + TAPS - 1)
    else:
        rows = pl.ds(b * STEP + TAPS - 1, STEP)
    return pltpu.make_async_copy(frames_hbm.at[rows], frames_ref.at[rows], sem.at[b])


def filter_pair(pair, first, count, raw_ref, window_ref, gain_ref, folded_ref):
    for side in range(2):
        i = 2 * pair + side
        gain = gain_ref[i] * SCALE
        for block in range(HALF // 128):
            acc = []
            for half in range(2):
                tile = half * (HALF // 128) + block
                lanes = slice(tile * 128, tile * 128 + 128)
                total = None
                for tap in range(TAPS):
                    weight = window_ref[tap : tap + 1, lanes] * gain
                    term = weight * raw_ref[tile, pl.ds((first + tap) * PITCH + i, count, stride=PITCH)]
                    total = term if total is None else total + term
                acc.append(total)
            lanes = slice(block * 128, block * 128 + 128)
            mine = slice(i * SPECTRA + first, i * SPECTRA + first + count)
            folded_ref[0, mine, lanes] = (acc[0] + acc[1]).astype(BF16)
            folded_ref[1, mine, lanes] = (acc[0] - acc[1]).astype(BF16)


def transform_pair(pair, parity, table_refs, folded_ref, turned_refs):
    rows = folded_ref[parity, pair * 256 : pair * 256 + 256, :]
    spec = lax.dot_general(table_refs[parity][...], rows, NT, preferred_element_type=F32)
    for m in range(PER):
        for ri in range(2):
            base = (m * 2 + ri) * DEVICES
            for side in range(2):
                turned_refs[parity][m, ri, pl.ds(2 * pair + side, DEVICES, stride=PITCH)] = (
                    spec[base : base + DEVICES, side * SPECTRA : (side + 1) * SPECTRA]
                )


def pack(c, turned_refs, sent_refs, out_hbm, out_sem):
    turned_ref = turned_refs[c // PER]
    sent_ref = sent_refs[c // PER]
    m = c % PER
    for owner in range(DEVICES):
        for ri in range(2):
            rows = turned_ref[m, ri, owner * PITCH : owner * PITCH + LOCAL]
            sent_ref[owner, m, :, ri * SPECTRA : (ri + 1) * SPECTRA] = rows.astype(BF16)
    store = pltpu.make_async_copy(sent_ref.at[:, m], out_hbm.at[:, c], out_sem.at[c])
    store.start()
    return store


def transform_kernel(
    frames_hbm, window_hbm, coarse_hbm, fine_hbm, table_hbm, gain_hbm, out_hbm,
    gain_ref, frames_ref, window_ref, coarse_ref, fine_ref, table_even, table_odd, raw_ref, folded_ref, turned_even, turned_odd, sent_even, sent_odd, frame_sem, sem, out_sem,
):
    turned_refs = (turned_even, turned_odd)
    sent_refs = (sent_even, sent_odd)
    table_refs = (table_even, table_odd)
    small = [
        pltpu.make_async_copy(coarse_hbm, coarse_ref, sem.at[3]),
        pltpu.make_async_copy(fine_hbm, fine_ref, sem.at[4]),
    ]
    for copy in small:
        copy.start()
    window_load = pltpu.make_async_copy(window_hbm, window_ref, sem.at[0])
    window_load.start()
    gain_load = pltpu.make_async_copy(gain_hbm, gain_ref, sem.at[2])
    gain_load.start()
    loads = [frames_of(b, frames_hbm, frames_ref, frame_sem) for b in range(SPECTRA // STEP)]
    for load in loads:
        load.start()
    table_load = pltpu.make_async_copy(table_hbm, table_odd, sem.at[1])
    table_load.start()
    for copy in small:
        copy.wait()
    even_table(coarse_ref, fine_ref, table_even)
    window_load.wait()
    gain_load.wait()
    for b, load in enumerate(loads):
        load.wait()
        first = b * STEP + TAPS - 1 if b else 0
        for f in range(first, (b + 1) * STEP + TAPS - 1):
            for tile in range(FRAME // 128):
                raw_ref[tile, f * PITCH : f * PITCH + LOCAL] = frames_ref[f, :, tile * 128 : tile * 128 + 128].astype(F32)
        if (b + 1) % 2 == 0:
            filter_pair(0, (b + 1 - 2) * STEP, 2 * STEP, raw_ref, window_ref, gain_ref, folded_ref)
    table_load.wait()
    stores = []
    for pair in range(LOCAL // 2):
        transform_pair(pair, 0, table_refs, folded_ref, turned_refs)
        if pair + 1 < LOCAL // 2:
            filter_pair(pair + 1, 0, SPECTRA, raw_ref, window_ref, gain_ref, folded_ref)
        else:
            for c in range(PER):
                stores.append(pack(c, turned_refs, sent_refs, out_hbm, out_sem))
        transform_pair(pair, 1, table_refs, folded_ref, turned_refs)
    for c in range(PER, OWNED):
        stores.append(pack(c, turned_refs, sent_refs, out_hbm, out_sem))
    for store in stores:
        store.wait()


def prepare(c, spectra_ref, volt_ref, turn_ref):
    slot = c % 2
    volt = spectra_ref[:, c].reshape(INPUTS, 2 * SPECTRA)
    volt_ref[slot] = volt
    turn_ref[slot, :, :SPECTRA] = -volt[:, SPECTRA:]
    turn_ref[slot, :, SPECTRA:] = volt[:, :SPECTRA]
    wide = volt.astype(F32)
    part = jnp.sum((wide * wide).reshape(8, INPUTS // 64, 8, 2 * SPECTRA), axis=1)
    power = jnp.sum(jnp.sum(part, axis=0), keepdims=True) * (1.0 / (SCALE * SCALE))
    return (1.0 / (power / (INPUTS * SPECTRA) + 1e-06)) * (1.0 / (SCALE * SCALE * SPECTRA))


def pair_of(row, col):
    return row * NBLK - row * (row - 1) // 2 + col - row


def gram_kernel(spectra_ref, out_hbm, volt_ref, turn_ref, tiles_ref, sem):
    scale = prepare(0, spectra_ref, volt_ref, turn_ref)
    stores = []
    for c in range(OWNED):
        slot = c % 2
        channel = 2 * (c % PER) + c // PER
        following = None
        for cols in reversed(range(NBLK // 2)):
            height = (2 * cols + 2) * BLOCK
            at = slice(cols * 256, cols * 256 + 256)
            for ri, right_ref in enumerate((volt_ref, turn_ref)):
                tiles = lax.dot_general(volt_ref[slot, :height], right_ref[slot, at], NT, preferred_element_type=F32)
                for row in range(2 * cols + 2):
                    for side in range(2):
                        col = 2 * cols + side
                        if col >= row:
                            tile = tiles[row * BLOCK : (row + 1) * BLOCK, side * BLOCK : (side + 1) * BLOCK]
                            tiles_ref[c, pair_of(row, col), ri] = (tile * scale).astype(BF16)
            if following is None and c + 1 < OWNED:
                following = prepare(c + 1, spectra_ref, volt_ref, turn_ref)
        stores.append(pltpu.make_async_copy(tiles_ref.at[c], out_hbm.at[channel], sem.at[c]))
        stores[-1].start()
        scale = following
    for store in stores:
        store.wait()


def gram(received):
    shape = (OWNED, NBLK * (NBLK + 1) // 2, 2, BLOCK, BLOCK)
    return pl.pallas_call(
        gram_kernel,
        name="gram",
        in_specs=[pl.BlockSpec(memory_space=pltpu.VMEM)],
        out_specs=pl.BlockSpec(memory_space=pltpu.HBM),
        out_shape=jax.ShapeDtypeStruct(shape, BF16),
        scratch_shapes=[
            pltpu.VMEM((2, INPUTS, 2 * SPECTRA), BF16),
            pltpu.VMEM((2, INPUTS, 2 * SPECTRA), BF16),
            pltpu.VMEM(shape, BF16),
            pltpu.SemaphoreType.DMA((OWNED,)),
        ],
        compiler_params=pltpu.CompilerParams(vmem_limit_bytes=48 << 20),
    )(received)


def local(samples, input_gain):
    frames = samples.reshape(LOCAL, SPECTRA + TAPS - 1, FRAME).transpose(1, 0, 2)
    table = jnp.asarray(odd_table())
    coarse, fine = (jnp.asarray(t) for t in twiddles())
    window = jnp.asarray(pfb_window())
    rows = LOCAL * SPECTRA
    hbm = pl.BlockSpec(memory_space=pltpu.HBM)
    outgoing = pl.pallas_call(
        transform_kernel,
        name="transform",
        in_specs=[hbm] * 6,
        out_specs=hbm,
        out_shape=jax.ShapeDtypeStruct((DEVICES, OWNED, LOCAL, 2 * SPECTRA), BF16),
        scratch_shapes=[
            pltpu.SMEM((LOCAL,), F32),
            pltpu.VMEM(frames.shape, BF16),
            pltpu.VMEM(window.shape, F32),
            pltpu.VMEM(coarse.shape, F32),
            pltpu.VMEM(fine.shape, F32),
            *[pltpu.VMEM(table.shape, BF16)] * 2,
            pltpu.VMEM((FRAME // 128, pl.cdiv(frames.shape[0] * PITCH, 8) * 8, 128), F32),
            pltpu.VMEM((2, rows, HALF), BF16),
            *[pltpu.VMEM((PER, 2, DEVICES * PITCH, SPECTRA), F32)] * 2,
            *[pltpu.VMEM((DEVICES, PER, LOCAL, 2 * SPECTRA), BF16)] * 2,
            pltpu.SemaphoreType.DMA((SPECTRA // STEP,)),
            pltpu.SemaphoreType.DMA((5,)),
            pltpu.SemaphoreType.DMA((OWNED,)),
        ],
        compiler_params=pltpu.CompilerParams(vmem_limit_bytes=56 << 20),
    )(frames, window, coarse, fine, table, input_gain)
    return gram(lax.all_to_all(outgoing, "dev", split_axis=0, concat_axis=0, tiled=True))


def solution(mesh):
    in_specs = (P("dev", None), P("dev"))
    out_specs = P("dev", None, None, None, None)
    return jax.shard_map(local, mesh=mesh, in_specs=in_specs, out_specs=out_specs, check_vma=False)
```

```python
import math

import jax
import jax.numpy as jnp
import numpy as np
from jax import lax
from jax.experimental import pallas as pl
from jax.experimental.pallas import tpu as pltpu
from jax.sharding import PartitionSpec as P

INPUTS = 1024
FRAME = 1536
TAPS = 4
SPECTRA = 128
BLOCK = 128
CHANNELS = 768
DEVICES = 128
LOCAL = INPUTS // DEVICES
OWNED = CHANNELS // DEVICES
HALF = FRAME // 2
NBLK = INPUTS // BLOCK
PER = OWNED // 2
STEP = 32
PITCH = 9
SCALE = 1024.0
F32 = jnp.float32
BF16 = jnp.bfloat16
NT = (((1,), (1,)), ((), ()))


def pfb_window():
    total = TAPS * FRAME
    position = np.arange(total, dtype=np.float64)
    centred = (position - total / 2 + 0.5) / FRAME
    taper = 0.54 - 0.46 * np.cos(2.0 * math.pi * position / (total - 1))
    return (np.sinc(centred) * taper).reshape(TAPS, FRAME).astype(np.float32)


def twiddles():
    owner = np.outer(np.arange(DEVICES), np.arange(256)) % 256 * (2.0 * math.pi / 256)
    own = np.outer(np.arange(OWNED), np.arange(HALF)) % FRAME * (2.0 * math.pi / FRAME)
    coarse = np.stack([np.cos(owner), -np.sin(owner)]) / math.sqrt(FRAME)
    fine = np.stack([np.cos(own), -np.sin(own)])
    return coarse.astype(np.float32), fine.astype(np.float32)


def odd_table():
    m, owner = np.meshgrid(np.arange(PER), np.arange(DEVICES), indexing="ij")
    channel = OWNED * owner + 2 * m + 1
    angle = 2.0 * math.pi / FRAME * (channel[..., None] * np.arange(HALF) % FRAME)
    table = np.stack([np.cos(angle), -np.sin(angle)], axis=1) / math.sqrt(FRAME)
    return table.reshape(CHANNELS, HALF).astype(np.float32).astype(jnp.bfloat16)


def even_table(coarse_ref, fine_ref, table_ref):
    group = 32
    for top in range(0, DEVICES, group):
        re = coarse_ref[0, top : top + group]
        im = coarse_ref[1, top : top + group]
        for block in range(HALF // 256):
            lanes = slice(block * 256, block * 256 + 256)
            for m in range(PER):
                at = m * 2 * DEVICES + top
                if m == 0:
                    table_ref[at : at + group, lanes] = re.astype(BF16)
                    table_ref[at + DEVICES : at + DEVICES + group, lanes] = im.astype(BF16)
                    continue
                fre = fine_ref[0, 2 * m : 2 * m + 1, lanes]
                fim = fine_ref[1, 2 * m : 2 * m + 1, lanes]
                table_ref[at : at + group, lanes] = (re * fre - im * fim).astype(BF16)
                table_ref[at + DEVICES : at + DEVICES + group, lanes] = (re * fim + im * fre).astype(BF16)


def frames_of(b, frames_hbm, frames_ref, sem):
    if b == 0:
        rows = pl.ds(0, STEP + TAPS - 1)
    else:
        rows = pl.ds(b * STEP + TAPS - 1, STEP)
    return pltpu.make_async_copy(frames_hbm.at[rows], frames_ref.at[rows], sem.at[b])


def filter_pair(pair, first, count, raw_ref, window_ref, gain_ref, folded_ref):
    for side in range(2):
        i = 2 * pair + side
        gain = gain_ref[i] * SCALE
        for block in range(HALF // 128):
            acc = []
            for half in range(2):
                tile = half * (HALF // 128) + block
                lanes = slice(tile * 128, tile * 128 + 128)
                total = None
                for tap in range(TAPS):
                    weight = window_ref[tap : tap + 1, lanes] * gain
                    term = weight * raw_ref[tile, pl.ds((first + tap) * PITCH + i, count, stride=PITCH)]
                    total = term if total is None else total + term
                acc.append(total)
            lanes = slice(block * 128, block * 128 + 128)
            mine = slice(i * SPECTRA + first, i * SPECTRA + first + count)
            folded_ref[0, mine, lanes] = (acc[0] + acc[1]).astype(BF16)
            folded_ref[1, mine, lanes] = (acc[0] - acc[1]).astype(BF16)


def transform_pair(pair, parity, table_refs, folded_ref, turned_refs):
    rows = folded_ref[parity, pair * 256 : pair * 256 + 256, :]
    spec = lax.dot_general(table_refs[parity][...], rows, NT, preferred_element_type=F32)
    for m in range(PER):
        for ri in range(2):
            base = (m * 2 + ri) * DEVICES
            for side in range(2):
                turned_refs[parity][m, ri, pl.ds(2 * pair + side, DEVICES, stride=PITCH)] = (
                    spec[base : base + DEVICES, side * SPECTRA : (side + 1) * SPECTRA]
                )


def pack(c, turned_refs, sent_refs, out_hbm, out_sem):
    turned_ref = turned_refs[c // PER]
    sent_ref = sent_refs[c // PER]
    m = c % PER
    for owner in range(DEVICES):
        for ri in range(2):
            rows = turned_ref[m, ri, owner * PITCH : owner * PITCH + LOCAL]
            sent_ref[owner, m, :, ri * SPECTRA : (ri + 1) * SPECTRA] = rows.astype(BF16)
    store = pltpu.make_async_copy(sent_ref.at[:, m], out_hbm.at[:, c], out_sem.at[c])
    store.start()
    return store


def transform_kernel(
    frames_hbm, window_hbm, coarse_hbm, fine_hbm, table_hbm, gain_hbm, out_hbm,
    gain_ref, frames_ref, window_ref, coarse_ref, fine_ref, table_even, table_odd, raw_ref, folded_ref, turned_even, turned_odd, sent_even, sent_odd, frame_sem, sem, out_sem,
):
    turned_refs = (turned_even, turned_odd)
    sent_refs = (sent_even, sent_odd)
    table_refs = (table_even, table_odd)
    small = [
        pltpu.make_async_copy(coarse_hbm, coarse_ref, sem.at[3]),
        pltpu.make_async_copy(fine_hbm, fine_ref, sem.at[4]),
    ]
    for copy in small:
        copy.start()
    window_load = pltpu.make_async_copy(window_hbm, window_ref, sem.at[0])
    window_load.start()
    gain_load = pltpu.make_async_copy(gain_hbm, gain_ref, sem.at[2])
    gain_load.start()
    loads = [frames_of(b, frames_hbm, frames_ref, frame_sem) for b in range(SPECTRA // STEP)]
    for load in loads:
        load.start()
    table_load = pltpu.make_async_copy(table_hbm, table_odd, sem.at[1])
    table_load.start()
    for copy in small:
        copy.wait()
    even_table(coarse_ref, fine_ref, table_even)
    window_load.wait()
    gain_load.wait()
    for b, load in enumerate(loads):
        load.wait()
        first = b * STEP + TAPS - 1 if b else 0
        for f in range(first, (b + 1) * STEP + TAPS - 1):
            for tile in range(FRAME // 128):
                raw_ref[tile, f * PITCH : f * PITCH + LOCAL] = frames_ref[f, :, tile * 128 : tile * 128 + 128].astype(F32)
        if (b + 1) % 2 == 0:
            filter_pair(0, (b + 1 - 2) * STEP, 2 * STEP, raw_ref, window_ref, gain_ref, folded_ref)
    table_load.wait()
    stores = []
    for pair in range(LOCAL // 2):
        transform_pair(pair, 0, table_refs, folded_ref, turned_refs)
        if pair + 1 < LOCAL // 2:
            filter_pair(pair + 1, 0, SPECTRA, raw_ref, window_ref, gain_ref, folded_ref)
        else:
            for c in range(PER):
                stores.append(pack(c, turned_refs, sent_refs, out_hbm, out_sem))
        transform_pair(pair, 1, table_refs, folded_ref, turned_refs)
    for c in range(PER, OWNED):
        stores.append(pack(c, turned_refs, sent_refs, out_hbm, out_sem))
    for store in stores:
        store.wait()


def prepare(c, spectra_ref, volt_ref, turn_ref):
    slot = c % 2
    volt = spectra_ref[:, c].reshape(INPUTS, 2 * SPECTRA)
    volt_ref[slot] = volt
    turn_ref[slot, :, :SPECTRA] = -volt[:, SPECTRA:]
    turn_ref[slot, :, SPECTRA:] = volt[:, :SPECTRA]
    wide = volt.astype(F32)
    part = jnp.sum((wide * wide).reshape(8, INPUTS // 64, 8, 2 * SPECTRA), axis=1)
    power = jnp.sum(jnp.sum(part, axis=0), keepdims=True) * (1.0 / (SCALE * SCALE))
    return (1.0 / (power / (INPUTS * SPECTRA) + 1e-06)) * (1.0 / (SCALE * SCALE * SPECTRA))


def pair_of(row, col):
    return row * NBLK - row * (row - 1) // 2 + col - row


def gram_kernel(spectra_ref, out_hbm, volt_ref, turn_ref, tiles_ref, sem):
    scale = prepare(0, spectra_ref, volt_ref, turn_ref)
    stores = []
    for c in range(OWNED):
        slot = c % 2
        channel = 2 * (c % PER) + c // PER
        following = None
        for cols in reversed(range(NBLK // 2)):
            height = (2 * cols + 2) * BLOCK
            at = slice(cols * 256, cols * 256 + 256)
            for ri, right_ref in enumerate((volt_ref, turn_ref)):
                tiles = lax.dot_general(volt_ref[slot, :height], right_ref[slot, at], NT, preferred_element_type=F32)
                for row in range(2 * cols + 2):
                    for side in range(2):
                        col = 2 * cols + side
                        if col >= row:
                            tile = tiles[row * BLOCK : (row + 1) * BLOCK, side * BLOCK : (side + 1) * BLOCK]
                            tiles_ref[c, pair_of(row, col), ri] = (tile * scale).astype(BF16)
            if cols == 1 and c + 1 < OWNED:
                following = prepare(c + 1, spectra_ref, volt_ref, turn_ref)
        stores.append(pltpu.make_async_copy(tiles_ref.at[c], out_hbm.at[channel], sem.at[c]))
        stores[-1].start()
        scale = following
    for store in stores:
        store.wait()


def gram(received):
    shape = (OWNED, NBLK * (NBLK + 1) // 2, 2, BLOCK, BLOCK)
    return pl.pallas_call(
        gram_kernel,
        name="gram",
        in_specs=[pl.BlockSpec(memory_space=pltpu.VMEM)],
        out_specs=pl.BlockSpec(memory_space=pltpu.HBM),
        out_shape=jax.ShapeDtypeStruct(shape, BF16),
        scratch_shapes=[
            pltpu.VMEM((2, INPUTS, 2 * SPECTRA), BF16),
            pltpu.VMEM((2, INPUTS, 2 * SPECTRA), BF16),
            pltpu.VMEM(shape, BF16),
            pltpu.SemaphoreType.DMA((OWNED,)),
        ],
        compiler_params=pltpu.CompilerParams(vmem_limit_bytes=48 << 20),
    )(received)


def local(samples, input_gain):
    frames = samples.reshape(LOCAL, SPECTRA + TAPS - 1, FRAME).transpose(1, 0, 2)
    table = jnp.asarray(odd_table())
    coarse, fine = (jnp.asarray(t) for t in twiddles())
    window = jnp.asarray(pfb_window())
    rows = LOCAL * SPECTRA
    hbm = pl.BlockSpec(memory_space=pltpu.HBM)
    outgoing = pl.pallas_call(
        transform_kernel,
        name="transform",
        in_specs=[hbm] * 6,
        out_specs=hbm,
        out_shape=jax.ShapeDtypeStruct((DEVICES, OWNED, LOCAL, 2 * SPECTRA), BF16),
        scratch_shapes=[
            pltpu.SMEM((LOCAL,), F32),
            pltpu.VMEM(frames.shape, BF16),
            pltpu.VMEM(window.shape, F32),
            pltpu.VMEM(coarse.shape, F32),
            pltpu.VMEM(fine.shape, F32),
            *[pltpu.VMEM(table.shape, BF16)] * 2,
            pltpu.VMEM((FRAME // 128, pl.cdiv(frames.shape[0] * PITCH, 8) * 8, 128), F32),
            pltpu.VMEM((2, rows, HALF), BF16),
            *[pltpu.VMEM((PER, 2, DEVICES * PITCH, SPECTRA), F32)] * 2,
            *[pltpu.VMEM((DEVICES, PER, LOCAL, 2 * SPECTRA), BF16)] * 2,
            pltpu.SemaphoreType.DMA((SPECTRA // STEP,)),
            pltpu.SemaphoreType.DMA((5,)),
            pltpu.SemaphoreType.DMA((OWNED,)),
        ],
        compiler_params=pltpu.CompilerParams(vmem_limit_bytes=56 << 20),
    )(frames, window, coarse, fine, table, input_gain)
    return gram(lax.all_to_all(outgoing, "dev", split_axis=0, concat_axis=0, tiled=True))


def solution(mesh):
    in_specs = (P("dev", None), P("dev"))
    out_specs = P("dev", None, None, None, None)
    return jax.shard_map(local, mesh=mesh, in_specs=in_specs, out_specs=out_specs, check_vma=False)
```
